512 devices in a mesh: lat: 32 (over x, z), lev: 16 (over y, core).
Axes of the slice: x: 4, y: 8, z: 8, core: 2. Of those that a mesh axis runs over, the one named last changes fastest.
Arguments:
- delta_p: float32 [64, 256, 1536], P('lev', 'lat'), may hold values from 0.5 to 1.5
- wind_u: float32 [64, 256, 1536], P('lev', 'lat'), may hold values from -6 to 6
- wind_v: float32 [64, 256, 1536], P('lev', 'lat'), may hold values from -6 to 6
- potential_temp: float32 [64, 256, 1536], P('lev', 'lat'), may hold values from 0.8 to 1.6
- tracer: float32 [64, 256, 1536], P('lev', 'lat'), may hold values from 0 to 1
- courant_north: float32 [64, 256, 1536], P('lev', 'lat'), may hold values from -0.3 to 0.3
- courant_east: float32 [64, 256, 1536], P('lev', 'lat'), may hold values from -0.15 to 0.15
Outputs:
- remapped_dp: float32 [64, 256, 1536], P('lev', 'lat')
- remapped_u: float32 [64, 256, 1536], P('lev', 'lat')
- remapped_v: float32 [64, 256, 1536], P('lev', 'lat')
- remapped_theta: float32 [64, 256, 1536], P('lev', 'lat')
- remapped_tracer: float32 [64, 256, 1536], P('lev', 'lat')
The draws below stay inside these ranges and needn't reach their ends.
All inputs are finite; a program needn't handle non-finite values.
Results may differ from the reference program's by a relative error of at most 0.0003.
Values sent between devices are 32-bit elements; how exact they have to be, the bound alone decides.
No kernel may reach another device: no remote copies, remote signals or barrier semaphores. Data moves between devices by JAX's collectives and lax.ppermute only.
A program may use at most 64 MiB of HBM per device.

```python
import jax
import jax.numpy as jnp
from jax import lax

NLON = 1536
STEPS = 3
NLAT = 256
NLEV = 64


def block_levels(own_key, extent, cuts, least, high):
    loudness, own = 1.0, jax.random.fold_in(own_key, 6)
    for dim, parts in cuts:
        heights = jnp.exp(jax.random.uniform(jax.random.fold_in(own, dim), (parts,), jnp.float32, least / len(cuts), high / len(cuts)))
        loudness = loudness * jnp.repeat(heights, extent[dim] // parts).reshape([-1 if axis == dim else 1 for axis in range(len(extent))])
    return loudness


def bell_draw(rng, extent, width, reach, cuts=(), kind=jnp.bfloat16):
    values = width * jax.random.normal(rng, extent, jnp.float32)
    if cuts:
        values = values * block_levels(rng, extent, cuts, -0.22, 0.18)
    return jnp.clip(values, -reach, reach).astype(kind)


def setup_inputs(seed: int = 0) -> dict:
    splits = jax.random.split(jax.random.key(seed), 8)
    delta_p = jnp.clip(0.5 + 1.0 * jax.random.uniform(splits[0], (NLEV, NLAT, NLON), jnp.float32) ** block_levels(splits[0], (NLEV, NLAT, NLON), ((0, 16), (1, 32)), -0.2, 0.2), 0.5, 1.5)
    wind_u = bell_draw(splits[1], (NLEV, NLAT, NLON), 1.0, 6.0, ((0, 16), (1, 32)), jnp.float32)
    wind_v = bell_draw(splits[2], (NLEV, NLAT, NLON), 1.0, 6.0, ((0, 16), (1, 32)), jnp.float32)
    potential_temp = jnp.clip(0.8 + 0.8 * jax.random.uniform(splits[3], (NLEV, NLAT, NLON), jnp.float32) ** block_levels(splits[3], (NLEV, NLAT, NLON), ((0, 16), (1, 32)), -0.2, 0.2), 0.8, 1.6)
    tracer = jnp.clip(1.0 * jax.random.uniform(splits[4], (NLEV, NLAT, NLON), jnp.float32) ** block_levels(splits[4], (NLEV, NLAT, NLON), ((0, 16), (1, 32)), -0.2, 0.2), 0.0, 1.0)
    courant_north = jnp.clip(jax.random.uniform(splits[5], (NLEV, NLAT, NLON), jnp.float32, -0.3, 0.3) * block_levels(splits[5], (NLEV, NLAT, NLON), ((0, 16), (1, 32)), -0.4, 0.0), -0.3, 0.3)
    courant_east = jnp.clip(jax.random.uniform(splits[6], (NLEV, NLAT, NLON), jnp.float32, -0.15, 0.15) * block_levels(splits[6], (NLEV, NLAT, NLON), ((0, 16), (1, 32)), -0.4, 0.0), -0.15, 0.15)
    return dict(delta_p=delta_p, wind_u=wind_u, wind_v=wind_v, potential_temp=potential_temp, tracer=tracer, courant_north=courant_north, courant_east=courant_east)


ptop_value = 1.0
push_coef = 0.5


def upwind(speed, upstream_a, upstream_b):
    return jnp.maximum(speed, 0.0) * upstream_a + jnp.minimum(speed, 0.0) * upstream_b


def remap_columns(masses, fields):
    level_count = masses.shape[0]
    layer_top = ptop_value + (jnp.cumsum(masses, axis=0) - masses)
    thickness = jnp.sum(masses, axis=0) / level_count
    target_ids = jnp.arange(1, level_count + 1).astype(jnp.float32)
    targets = ptop_value + target_ids[:, None] * thickness[None, :]
    target_blocks = targets.reshape(level_count // 8, 8, targets.shape[1])

    def cumulate(target_block):
        fraction = jnp.clip((target_block[:, None, :] - layer_top[None]) / masses[None], 0.0, 1.0)
        return jnp.sum(fraction[None] * fields[:, None], axis=2)

    cumulative = lax.map(cumulate, target_blocks)
    cumulative = jnp.moveaxis(cumulative, 1, 0).reshape(fields.shape[0], level_count, targets.shape[1])
    shifted = jnp.concatenate([jnp.zeros_like(cumulative[:, :1]), cumulative[:, :-1]], axis=1)
    return thickness, (cumulative - shifted) / thickness[None, None, :]


def advance(state, north_c, south_c, east_c):
    masses = state[0]
    layer_top = ptop_value + (jnp.cumsum(masses, axis=0) - masses)
    log_middle = jnp.log(layer_top + 0.5 * masses)
    accel = -push_coef * state[3] * (jnp.roll(log_middle, -1, axis=-1) - jnp.roll(log_middle, 1, axis=-1))
    state = jnp.concatenate([state[:1], state[1:2] + accel[None], state[2:]], axis=0)
    padded = jnp.pad(state, ((0, 0), (0, 0), (1, 1), (0, 0)))
    centre = padded[:, :, 1:-1]
    north_rows = padded[:, :, 2:]
    south_rows = padded[:, :, :-2]
    north_flux = upwind(north_c, centre, north_rows)
    south_flux = upwind(south_c, south_rows, centre)
    east_flux = upwind(east_c, centre, jnp.roll(centre, -1, axis=-1))
    west_flux = jnp.roll(east_flux, 1, axis=-1)
    return centre - (north_flux - south_flux) - (east_flux - west_flux)


def reference(delta_p, wind_u, wind_v, potential_temp, tracer, courant_north, courant_east):
    row_ids = jnp.arange(NLAT, dtype=jnp.int32)
    north_c = jnp.where((row_ids < NLAT - 1)[None, :, None], courant_north, 0.0)
    south_c = jnp.concatenate([jnp.zeros_like(north_c[:, :1]), north_c[:, :-1]], axis=1)
    state = jnp.stack([delta_p, wind_u * delta_p, wind_v * delta_p, potential_temp * delta_p, tracer * delta_p])
    for sweep_id in range(STEPS):
        state = advance(state, north_c, south_c, courant_east)
    by_rows = jnp.moveaxis(state, 2, 0)

    def remap_row(row_state):
        thickness, values = remap_columns(row_state[0], row_state[1:])
        filled = jnp.broadcast_to(thickness[None, None], (1, values.shape[1], values.shape[2]))
        return jnp.concatenate([filled, values], axis=0)

    result = jnp.moveaxis(lax.map(remap_row, by_rows), 0, 2)
    return result[0], result[1], result[2], result[3], result[4]
```

```python
import functools

import jax
import jax.numpy as jnp
from jax import lax
from jax.experimental import pallas as pl
from jax.experimental.pallas import tpu as pltpu
from jax.sharding import PartitionSpec as P

STEPS = 3
LEVELS = 64
OWN = 4
GROUP = 16
WIDTH = 96
LANES = 128
TILES = 12
FIELDS = 5
CARRIED = 7
VMEM = pltpu.VMEM


def lane_ids():
    return lax.broadcasted_iota(jnp.int32, (8, LANES), 1)


def row_ids():
    return lax.broadcasted_iota(jnp.int32, (8, LANES), 0)


def pack_kernel(last_ref, dp_ref, u_ref, v_ref, th_ref, tr_ref, cn_ref, ce_ref, out_ref):
    lane = lane_ids()
    closed = jnp.logical_and(last_ref[0] > 0, row_ids() == 7)

    def level(l, _):
        for field, ref in enumerate((dp_ref, u_ref, v_ref, th_ref, tr_ref, cn_ref, ce_ref)):
            tiles = []
            for t in range(TILES):
                x = ref[l, :, t * LANES : (t + 1) * LANES]
                if 1 <= field <= 4:
                    x = x * dp_ref[l, :, t * LANES : (t + 1) * LANES]
                if field == 5:
                    x = jnp.where(closed, 0.0, x)
                tiles.append(x)
            for d in range(GROUP):
                first = d * WIDTH - 16
                a, off = first // LANES, first % LANES
                x = jnp.where(lane >= off, tiles[a % TILES], tiles[(a + 1) % TILES])
                out_ref[d, field * OWN + l] = x
        return 0

    lax.fori_loop(0, OWN, level, 0)


def pack(last, args):
    return pl.pallas_call(
        pack_kernel,
        out_shape=jax.ShapeDtypeStruct((GROUP, CARRIED * OWN, 8, LANES), jnp.float32),
        in_specs=[pl.BlockSpec(memory_space=pltpu.SMEM)] + [pl.BlockSpec(memory_space=VMEM)] * 7,
        out_specs=pl.BlockSpec(memory_space=VMEM),
        name="pack",
    )(last, *args)


def edges_kernel(x_ref, north_ref, south_ref):
    def group(g, _):
        for i in range(8):
            for f in range(CARRIED):
                at = (2 * g + i // OWN, f * OWN + i % OWN)
                north_ref[f, g, 3 * i : 3 * i + 3, :] = x_ref[at[0], at[1], 5:8, :]
                south_ref[f, g, 3 * i : 3 * i + 3, :] = x_ref[at[0], at[1], 0:3, :]
        return 0

    lax.fori_loop(0, 8, group, 0)


def edges(x):
    shape = jax.ShapeDtypeStruct((CARRIED, 8, 24, LANES), jnp.float32)
    return pl.pallas_call(
        edges_kernel,
        out_shape=(shape, shape),
        in_specs=[pl.BlockSpec(memory_space=VMEM)],
        out_specs=(pl.BlockSpec(memory_space=VMEM),) * 2,
        name="edges",
    )(x)


def up(pair, is_top):
    m, h = (pltpu.roll(x, 7, 0) for x in pair)
    return jnp.where(is_top, h, m), jnp.where(is_top, m, h)


def down(pair, is_bottom):
    m, h = (pltpu.roll(x, 1, 0) for x in pair)
    return jnp.where(is_bottom, h, m), jnp.where(is_bottom, m, h)


def advance_pair(x, cn, ce, masks, both):
    is_top, is_bottom = masks
    nxt = up(x, is_top)
    north = tuple(cn[0][p] * x[p] + cn[1][p] * nxt[p] for p in range(2))
    south = down(north, is_bottom)
    out = []
    for p in range(2 if both else 1):
        east = ce[0][p] * x[p] + ce[1][p] * pltpu.roll(x[p], LANES - 1, 1)
        west = pltpu.roll(east, 1, 1)
        out.append(x[p] - (north[p] - south[p]) - (east - west))
    return tuple(out)


def columns_kernel(x_ref, north_ref, south_ref, out_ref, halo, top, inverse, final):
    is_top, is_bottom = row_ids() == 7, row_ids() == 0
    masks = (is_top, is_bottom)
    halo[...] = jnp.zeros_like(halo)

    def group(g, runs):
        runs = list(runs)
        for i in range(8):
            for f in range(CARRIED):
                halo[f, i, 0:3, :] = north_ref[f, g, 3 * i : 3 * i + 3, :]
                halo[f, i, 5:8, :] = south_ref[f, g, 3 * i : 3 * i + 3, :]
        for i in range(8):
            state = [(x_ref[2 * g + i // OWN, f * OWN + i % OWN], halo[f, i]) for f in range(CARRIED)]
            cn, ce = (
                (tuple(jnp.maximum(c, 0.0) for c in pair), tuple(jnp.minimum(c, 0.0) for c in pair))
                for pair in state[FIELDS:]
            )
            state = state[:FIELDS]
            for step in range(STEPS):
                pushed = []
                for p in range(2):
                    run = runs[2 * step + p]
                    mass = state[0][p]
                    log_middle = jnp.log(run + 0.5 * mass)
                    slope = pltpu.roll(log_middle, LANES - 1, 1) - pltpu.roll(log_middle, 1, 1)
                    pushed.append(state[1][p] - 0.5 * state[3][p] * slope)
                    runs[2 * step + p] = run + mass
                state[1] = tuple(pushed)
                state = [advance_pair(x, cn, ce, masks, step < STEPS - 1) for x in state]
            at = 8 * g + i
            mass = state[0][0]
            top[at] = runs[-1]
            runs[-1] = runs[-1] + mass
            inverse[at] = 1.0 / mass
            for f in range(1, FIELDS):
                final[f - 1, at] = state[f][0]
        return tuple(runs)

    one = jnp.ones((8, LANES), jnp.float32)
    runs = lax.fori_loop(0, 8, group, (one,) * (2 * STEPS + 1))
    h = (runs[-1] - 1.0) * (1.0 / LEVELS)
    inverse_h = 1.0 / h

    def targets(kb, last):
        base = 1.0 + h * (8 * kb + 1).astype(jnp.float32)

        def layer(j, acc):
            inv = inverse[j]
            u = (base - top[j]) * inv
            stride = h * inv
            values = [final[f, j] for f in range(4)]
            acc = list(acc)
            for k in range(8):
                w = jnp.minimum(jnp.maximum(u, 0.0), 1.0)
                for f in range(4):
                    acc[4 * k + f] = acc[4 * k + f] + w * values[f]
                if k < 7:
                    u = u + stride
            return tuple(acc)

        acc = lax.fori_loop(0, LEVELS, layer, (jnp.zeros((8, LANES), jnp.float32),) * 32)
        for k in range(8):
            for f in range(4):
                below = acc[4 * (k - 1) + f] if k else last[f]
                out_ref[2 * kb + k // OWN, f * OWN + k % OWN] = (acc[4 * k + f] - below) * inverse_h
        return tuple(acc[28:])

    lax.fori_loop(0, 8, targets, (jnp.zeros((8, LANES), jnp.float32),) * 4)
    for d in range(GROUP):
        out_ref[d, 16] = h


def columns(x, north, south):
    return pl.pallas_call(
        columns_kernel,
        out_shape=jax.ShapeDtypeStruct((GROUP, 17, 8, LANES), jnp.float32),
        in_specs=[pl.BlockSpec(memory_space=VMEM)] * 3,
        out_specs=pl.BlockSpec(memory_space=VMEM),
        scratch_shapes=[
            VMEM((CARRIED, 8, 8, LANES), jnp.float32),
            VMEM((LEVELS, 8, LANES), jnp.float32),
            VMEM((LEVELS, 8, LANES), jnp.float32),
            VMEM((4, LEVELS, 8, LANES), jnp.float32),
        ],
        name="columns",
    )(x, north, south)


def unpack_kernel(x_ref, dp_ref, u_ref, v_ref, th_ref, tr_ref):
    lane = lane_ids()

    def merged(t, at):
        first = 4 * t // 3
        edge = (first + 1) * WIDTH - t * LANES
        if edge >= LANES:
            return x_ref[first, at]
        return jnp.where(lane < edge, x_ref[first, at], x_ref[first + 1, at])

    for t in range(TILES):
        span = slice(t * LANES, (t + 1) * LANES)
        h = merged(t, 16)
        for l in range(OWN):
            dp_ref[l, :, span] = h
            for f, ref in enumerate((u_ref, v_ref, th_ref, tr_ref)):
                ref[l, :, span] = merged(t, f * OWN + l)


def unpack(x):
    shape = jax.ShapeDtypeStruct((OWN, 8, TILES * LANES), jnp.float32)
    return pl.pallas_call(
        unpack_kernel,
        out_shape=(shape,) * 5,
        in_specs=[pl.BlockSpec(memory_space=VMEM)],
        out_specs=(pl.BlockSpec(memory_space=VMEM),) * 5,
        name="unpack",
    )(x)


def body(*args):
    lats = lax.axis_size("lat")
    last = (lax.axis_index("lat") == lats - 1).astype(jnp.int32).reshape(1)
    sent = pack(last, args)
    held = lax.all_to_all(sent, "lev", 0, 0, tiled=True)
    to_north, to_south = edges(held)
    forward = [(i, i + 1) for i in range(lats - 1)]
    backward = [(b, a) for a, b in forward]
    south = lax.ppermute(to_north, "lat", forward)
    north = lax.ppermute(to_south, "lat", backward)
    made = columns(held, north, south)
    back = lax.all_to_all(made, "lev", 0, 0, tiled=True)
    return tuple(unpack(back))


def solution(mesh):
    spec = P("lev", "lat", None)
    return jax.shard_map(body, mesh=mesh, in_specs=(spec,) * 7, out_specs=(spec,) * 5, check_vma=False)
```

```python
import functools

import jax
import jax.numpy as jnp
from jax import lax
from jax.experimental import pallas as pl
from jax.experimental.pallas import tpu as pltpu
from jax.sharding import PartitionSpec as P

STEPS = 3
LEVELS = 64
OWN = 4
GROUP = 16
WIDTH = 96
SPARE = 32
LANES = 128
TILES = 12
ROWS = 8
VMEM, SMEM = pltpu.VMEM, pltpu.SMEM

CHUNK_A = ((4, 4), (3, 3), (3, 3), (3, 4))
CHUNK_B = ((3, 3), (3, 3), (3, 3))


def places(chunk):
    at, out = 0, []
    for east, west in chunk:
        out.append([])
        for _ in range(OWN):
            out[-1].append((at, at + east))
            at += east + west
    assert at <= LANES
    return out


def tile_count(chunk):
    return 3 * len(chunk) + 1


def turn(x, by):
    by %= LANES
    return pltpu.roll(x, by, 1) if by else x


def iota(axis):
    return lax.broadcasted_iota(jnp.int32, (ROWS, LANES), axis)


def vmem(*shape):
    return jax.ShapeDtypeStruct(shape + (ROWS, LANES), jnp.float32)


IN_VMEM = pl.BlockSpec(memory_space=VMEM)
IN_SMEM = pl.BlockSpec(memory_space=SMEM)


def pack_kernel(last_ref, dp_ref, u_ref, v_ref, th_ref, tr_ref, cn_ref, ce_ref, a_ref, b_ref):
    lane = iota(1)
    closed = jnp.logical_and(last_ref[0] > 0, iota(0) == ROWS - 1)

    def load(ref, l, t):
        x = ref[l, :, t * LANES : (t + 1) * LANES]
        if any(ref is other for other in (u_ref, v_ref, th_ref, tr_ref)):
            x = x * dp_ref[l, :, t * LANES : (t + 1) * LANES]
        if ref is cn_ref:
            x = jnp.where(closed, 0.0, x)
        return x

    for chunk, refs, out_ref in (
        (CHUNK_A, (dp_ref, th_ref, cn_ref, ce_ref), a_ref),
        (CHUNK_B, (u_ref, v_ref, tr_ref), b_ref),
    ):
        where = places(chunk)
        for d in range(GROUP):
            gap = (3 * d + 3) % 4
            first = d * WIDTH - 16
            a, off = (first // LANES) % TILES, first % LANES
            slot = lane // SPARE
            rel = (lane - gap * SPARE) % LANES
            sides = jnp.zeros((ROWS, LANES), jnp.float32)
            for f, ref in enumerate(refs):
                east, west = chunk[f]
                own = []
                for l in range(OWN):
                    x = jnp.where(lane >= off, load(ref, l, a), load(ref, l, (a + 1) % TILES))
                    at_east, at_west = where[f][l]
                    sides = jnp.where(rel >= at_east, turn(x, at_east), sides)
                    sides = jnp.where(rel >= at_west, turn(x, at_west - (SPARE - west)), sides)
                    own.append(x)
                for i in range(3):
                    out_ref[d, 3 * f + i] = jnp.where(slot == gap, turn(own[3], -SPARE * (1 + i)), own[i])
            out_ref[d, 3 * len(chunk)] = sides


def pack(last, args):
    return pl.pallas_call(
        pack_kernel,
        out_shape=(vmem(GROUP, tile_count(CHUNK_A)), vmem(GROUP, tile_count(CHUNK_B))),
        in_specs=[IN_SMEM] + [IN_VMEM] * 7,
        out_specs=(IN_VMEM,) * 2,
        name="pack",
    )(last, *args)


def edges_kernel(chunk, outs, gap_ref, x_ref, *refs):
    north_ref, south_ref = refs[-2:]
    out_refs = [ref.at[k] for ref, n in zip(refs[:-2], outs) for k in range(n)]
    where = places(chunk)
    gap = gap_ref[0]
    rel = (iota(1) - gap * SPARE + LANES) % LANES
    quarter = rel // SPARE

    def group(g, _):
        for half in range(2):
            src = 2 * g + half
            sides = x_ref[src, 3 * len(chunk)]
            for f, (east, west) in enumerate(chunk):
                t = [x_ref[src, 3 * f + i] for i in range(3)]
                fourth = jnp.where(
                    quarter == 1,
                    turn(t[0], SPARE),
                    jnp.where(quarter == 2, turn(t[1], 2 * SPARE), turn(t[2], 3 * SPARE)),
                )
                for l, x in enumerate(t + [fourth]):
                    at_east, at_west = where[f][l]
                    x = jnp.where(quarter == 0, 0.0, x)
                    x = jnp.where(rel < east, turn(sides, -at_east), x)
                    in_west = jnp.logical_and(rel >= SPARE - west, rel < SPARE)
                    x = jnp.where(in_west, turn(sides, SPARE - west - at_west), x)
                    i = OWN * half + l
                    out_refs[f][OWN * src + l] = x
                    north_ref[f, g, 3 * i : 3 * i + 3, :] = x[5:8]
                    south_ref[f, g, 3 * i : 3 * i + 3, :] = x[0:3]
        return 0

    lax.fori_loop(0, 8, group, 0)


def edges(chunk, outs, gap, x):
    strip = jax.ShapeDtypeStruct((len(chunk), 8, 24, LANES), jnp.float32)
    return pl.pallas_call(
        functools.partial(edges_kernel, chunk, outs),
        out_shape=tuple(vmem(n, LEVELS) for n in outs) + (strip, strip),
        in_specs=[IN_SMEM, IN_VMEM],
        out_specs=(IN_VMEM,) * (len(outs) + 2),
        name="edges",
    )(gap, x)


def join_strips(north_ref, south_ref, halo_refs):
    for f, halo in enumerate(halo_refs):
        halo[...] = jnp.zeros(halo.shape, jnp.float32)

    def group(g, _):
        for f, halo in enumerate(halo_refs):
            for i in range(8):
                halo[8 * g + i, 0:3, :] = north_ref[f, g, 3 * i : 3 * i + 3, :]
                halo[8 * g + i, 5:8, :] = south_ref[f, g, 3 * i : 3 * i + 3, :]
        return 0

    lax.fori_loop(0, 8, group, 0)


def shifted(pair, by, edge):
    m, h = (pltpu.roll(x, by, 0) for x in pair)
    return jnp.where(edge, h, m), jnp.where(edge, m, h)


def coefficients(cn, ce, is_top, is_bottom):
    cs = shifted(cn, 1, is_bottom)
    out = []
    for p in range(2):
        cw = pltpu.roll(ce[p], 1, 1)
        south, west = jnp.maximum(cs[p], 0.0), jnp.maximum(cw, 0.0)
        north, east = jnp.maximum(-cn[p], 0.0), jnp.maximum(-ce[p], 0.0)
        own = 1.0 - jnp.maximum(cn[p], 0.0) + jnp.minimum(cs[p], 0.0)
        own = own - jnp.maximum(ce[p], 0.0) + jnp.minimum(cw, 0.0)
        out.append((own, north, south, east, west))
    return out


def transport(x, coefs, is_top, is_bottom, both):
    above, below = shifted(x, ROWS - 1, is_top), shifted(x, 1, is_bottom)
    out = []
    for p in range(2 if both else 1):
        own, north, south, east, west = coefs[p]
        sides = east * pltpu.roll(x[p], LANES - 1, 1) + west * pltpu.roll(x[p], 1, 1)
        out.append((own * x[p] + sides) + (north * above[p] + south * below[p]))
    return tuple(out)


def remap(count, out_ref, first_tile, prefix, final, top, inverse, h, low, high, gap):
    inverse_h = 1.0 / h
    slot = iota(1) // SPARE
    zero = jnp.zeros((ROWS, LANES), jnp.float32)

    def targets(kb, last):
        base = 1.0 + h * (8 * kb + 1).astype(jnp.float32)
        start = [prefix[f, low(kb)] for f in range(count)]

        def layers(jq, acc):
            acc = list(acc)
            for i in range(4):
                j = 4 * jq + i
                inv = inverse[j]
                u = (base - top[j]) * inv
                stride = h * inv
                values = [final[f, j] for f in range(count)]
                for k in range(8):
                    w = jnp.minimum(jnp.maximum(u, 0.0), 1.0)
                    for f in range(count):
                        acc[count * k + f] = acc[count * k + f] + w * values[f]
                    if k < 7:
                        u = u + stride
            return tuple(acc)

        acc = lax.fori_loop(2 * low(kb), 2 * high(kb), layers, tuple(start) * 8)
        for half in range(2):
            for f in range(count):
                own = []
                for l in range(OWN):
                    k = OWN * half + l
                    below = acc[count * (k - 1) + f] if k else last[f]
                    own.append((acc[count * k + f] - below) * inverse_h)
                for i in range(3):
                    moved = turn(own[3], -SPARE * (1 + i))
                    out_ref[2 * kb + half, first_tile + 3 * f + i] = jnp.where(slot == gap, moved, own[i])
        return tuple(acc[7 * count :])

    lax.fori_loop(0, 8, targets, (zero,) * count)


def first_kernel(
    gap_ref, x_ref, c_ref, north_ref, south_ref,
    out_ref, push_ref, halo_c_ref, top, inverse, h_ref, bound_ref,
    halo_x, final, prefix, least, most,
):
    gap = gap_ref[0]
    is_top, is_bottom = iota(0) == ROWS - 1, iota(0) == 0
    join_strips(north_ref, south_ref, [halo_x.at[0], halo_x.at[1], halo_c_ref.at[0], halo_c_ref.at[1]])

    def group(g, carried):
        prefix[0, g] = carried[-1]
        least[g] = carried[-2]

        def layers(i, carried):
            runs = list(carried)
            for n in range(2):
                j = 8 * g + 2 * i + n
                mass = (x_ref[0, j], halo_x[0, j])
                theta = (x_ref[1, j], halo_x[1, j])
                coefs = coefficients((c_ref[0, j], halo_c_ref[0, j]), (c_ref[1, j], halo_c_ref[1, j]), is_top, is_bottom)
                for step in range(STEPS):
                    for p in range(2):
                        run = runs[2 * step + p]
                        middle = jnp.log(run + 0.5 * mass[p])
                        slope = pltpu.roll(middle, LANES - 1, 1) - pltpu.roll(middle, 1, 1)
                        push_ref[j, 2 * step + p] = 0.5 * theta[p] * slope
                        runs[2 * step + p] = run + mass[p]
                    both = step < STEPS - 1
                    mass = transport(mass, coefs, is_top, is_bottom, both)
                    theta = transport(theta, coefs, is_top, is_bottom, both)
                top[j] = runs[-2]
                inverse[j] = 1.0 / mass[0]
                final[0, j] = theta[0]
                runs[-2] = runs[-2] + mass[0]
                runs[-1] = runs[-1] + theta[0]
            return tuple(runs)

        return lax.fori_loop(0, 4, layers, carried)

    one, zero = jnp.ones((ROWS, LANES), jnp.float32), jnp.zeros((ROWS, LANES), jnp.float32)
    carried = lax.fori_loop(0, 8, group, (one,) * (2 * STEPS + 1) + (zero,))
    prefix[0, 8] = carried[-1]
    h = (carried[-2] - 1.0) * (1.0 / LEVELS)
    h_ref[...] = h

    inside = iota(1) // SPARE != gap
    inverse_h = 1.0 / h
    for b in range(1, 8):
        begin = (least[b] - 1.0) * inverse_h
        most[b] = jnp.max(jnp.where(inside, begin, 0.0))
        least_b = jnp.min(jnp.where(inside, begin, 1.0 * LEVELS))
        for kb in range(8):
            done = (most[b] <= 8.0 * kb + 0.99).astype(jnp.int32)
            begun = (least_b < 8.0 * kb + 8.01).astype(jnp.int32)
            bound_ref[kb] = done if b == 1 else bound_ref[kb] + done
            bound_ref[8 + kb] = 1 + begun if b == 1 else bound_ref[8 + kb] + begun

    remap(1, out_ref, 0, prefix, final, top, inverse, h, lambda kb: bound_ref[kb], lambda kb: bound_ref[8 + kb], gap)


def first_columns(gap, x, c, north, south):
    return pl.pallas_call(
        first_kernel,
        out_shape=(
            vmem(GROUP, 3),
            vmem(LEVELS, 2 * STEPS),
            vmem(2, LEVELS),
            vmem(LEVELS),
            vmem(LEVELS),
            vmem(),
            jax.ShapeDtypeStruct((16,), jnp.int32),
        ),
        in_specs=[IN_SMEM] + [IN_VMEM] * 4,
        out_specs=(IN_VMEM,) * 6 + (IN_SMEM,),
        scratch_shapes=[
            VMEM((2, LEVELS, ROWS, LANES), jnp.float32),
            VMEM((1, LEVELS, ROWS, LANES), jnp.float32),
            VMEM((1, 9, ROWS, LANES), jnp.float32),
            VMEM((8, ROWS, LANES), jnp.float32),
            SMEM((8,), jnp.float32),
        ],
        name="first_columns",
    )(gap, x, c, north, south)


def second_kernel(
    gap_ref, bound_ref, x_ref, c_ref, halo_c_ref, push_ref, north_ref, south_ref, top, inverse, h_ref, theta_ref,
    out_ref, halo, final, prefix,
):
    gap = gap_ref[0]
    is_top, is_bottom = iota(0) == ROWS - 1, iota(0) == 0
    join_strips(north_ref, south_ref, [halo.at[f] for f in range(3)])

    def group(g, carried):
        for f in range(3):
            prefix[f, g] = carried[f]

        def layers(i, carried):
            sums = list(carried)
            for n in range(2):
                j = 8 * g + 2 * i + n
                coefs = coefficients((c_ref[0, j], halo_c_ref[0, j]), (c_ref[1, j], halo_c_ref[1, j]), is_top, is_bottom)
                for f in range(3):
                    x = (x_ref[f, j], halo[f, j])
                    for step in range(STEPS):
                        if f == 0:
                            x = tuple(x[p] - push_ref[j, 2 * step + p] for p in range(2))
                        x = transport(x, coefs, is_top, is_bottom, step < STEPS - 1)
                    final[f, j] = x[0]
                    sums[f] = sums[f] + x[0]
            return tuple(sums)

        return lax.fori_loop(0, 4, layers, carried)

    zero = jnp.zeros((ROWS, LANES), jnp.float32)
    carried = lax.fori_loop(0, 8, group, (zero,) * 3)
    for f in range(3):
        prefix[f, 8] = carried[f]
    h = h_ref[...]
    remap(3, out_ref, 0, prefix, final, top, inverse, h, lambda kb: bound_ref[kb], lambda kb: bound_ref[8 + kb], gap)
    for d in range(GROUP):
        for i in range(3):
            out_ref[d, 9 + i] = theta_ref[d, i]
        out_ref[d, 12] = h


def second_columns(gap, bound, *arrays):
    return pl.pallas_call(
        second_kernel,
        out_shape=vmem(GROUP, 13),
        in_specs=[IN_SMEM] * 2 + [IN_VMEM] * len(arrays),
        out_specs=IN_VMEM,
        scratch_shapes=[
            VMEM((3, LEVELS, ROWS, LANES), jnp.float32),
            VMEM((3, LEVELS, ROWS, LANES), jnp.float32),
            VMEM((3, 9, ROWS, LANES), jnp.float32),
        ],
        name="second_columns",
    )(gap, bound, *arrays)


def unpack_kernel(x_ref, dp_ref, u_ref, v_ref, th_ref, tr_ref):
    lane = iota(1)
    slot = lane // SPARE

    def fourth(d, f):
        gap = (3 * d + 3) % 4
        t = [turn(x_ref[d, 3 * f + i], SPARE * (1 + i)) for i in range(3)]
        return jnp.where(slot == (gap + 1) % 4, t[0], jnp.where(slot == (gap + 2) % 4, t[1], t[2]))

    def merged(t, get):
        d = 4 * t // 3
        edge = (d + 1) * WIDTH - t * LANES
        return get(d) if edge >= LANES else jnp.where(lane < edge, get(d), get(d + 1))

    spans = [slice(t * LANES, (t + 1) * LANES) for t in range(TILES)]
    for t, span in enumerate(spans):
        h = merged(t, lambda d: x_ref[d, 12])
        for l in range(OWN):
            dp_ref[l, :, span] = h
    for f, ref in enumerate((u_ref, v_ref, tr_ref, th_ref)):
        last = [fourth(d, f) for d in range(GROUP)]
        for t, span in enumerate(spans):
            for l in range(3):
                ref[l, :, span] = merged(t, lambda d: x_ref[d, 3 * f + l])
            ref[3, :, span] = merged(t, lambda d: last[d])


def unpack(x):
    shape = jax.ShapeDtypeStruct((OWN, ROWS, TILES * LANES), jnp.float32)
    return pl.pallas_call(
        unpack_kernel,
        out_shape=(shape,) * 5,
        in_specs=[IN_VMEM],
        out_specs=(IN_VMEM,) * 5,
        name="unpack",
    )(x)


def body(*args):
    lats = lax.axis_size("lat")
    last = (lax.axis_index("lat") == lats - 1).astype(jnp.int32).reshape(1)
    gap = ((3 * lax.axis_index("lev") + 3) % 4).astype(jnp.int32).reshape(1)
    forward = [(i, i + 1) for i in range(lats - 1)]
    backward = [(b, a) for a, b in forward]

    def across(x):
        return lax.all_to_all(x, "lev", 0, 0, tiled=True)

    def strips(to_north, to_south):
        return lax.ppermute(to_south, "lat", backward), lax.ppermute(to_north, "lat", forward)

    sent_a, sent_b = pack(last, args)
    x_a, courant, to_north, to_south = edges(CHUNK_A, (2, 2), gap, across(sent_a))
    sent_b, to_north, to_south = lax.optimization_barrier((sent_b, to_north, to_south))
    north_a, south_a = strips(to_north, to_south)
    x_b, to_north, to_south = edges(CHUNK_B, (3,), gap, across(sent_b))
    north_b, south_b = strips(to_north, to_south)
    theta, push, halo_c, top, inverse, h, bound = first_columns(gap, x_a, courant, north_a, south_a)
    made = second_columns(gap, bound, x_b, courant, halo_c, push, north_b, south_b, top, inverse, h, theta)
    return tuple(unpack(across(made)))


def solution(mesh):
    spec = P("lev", "lat", None)
    return jax.shard_map(body, mesh=mesh, in_specs=(spec,) * 7, out_specs=(spec,) * 5, check_vma=False)
```

```python
import functools

import jax
import jax.numpy as jnp
from jax import lax
from jax.experimental import pallas as pl
from jax.experimental.pallas import tpu as pltpu
from jax.sharding import PartitionSpec as P

STEPS = 3
LEVELS = 64
OWN = 4
GROUP = 16
WIDTH = 96
SPARE = 32
LANES = 128
TILES = 12
ROWS = 8
VMEM, SMEM = pltpu.VMEM, pltpu.SMEM

CHUNK_A = ((4, 4), (3, 3), (3, 3), (3, 4))
CHUNK_B = ((3, 3), (3, 3), (3, 3))


def places(chunk):
    at, out = 0, []
    for east, west in chunk:
        out.append([])
        for _ in range(OWN):
            out[-1].append((at, at + east))
            at += east + west
    assert at <= LANES
    return out


def tile_count(chunk):
    return 3 * len(chunk) + 1


def turn(x, by):
    by %= LANES
    return pltpu.roll(x, by, 1) if by else x


def iota(axis):
    return lax.broadcasted_iota(jnp.int32, (ROWS, LANES), axis)


def vmem(*shape):
    return VMEM(shape + (ROWS, LANES), jnp.float32)


IN_VMEM = pl.BlockSpec(memory_space=VMEM)
IN_SMEM = pl.BlockSpec(memory_space=SMEM)
GRANT = pltpu.CompilerParams(vmem_limit_bytes=16 << 20)


def near(*arrays):
    return tuple(pltpu.with_memory_space_constraint(x, VMEM) for x in arrays)


def pack_kernel(chunk, scaled, last_ref, *refs):
    lane = iota(1)
    slot = lane // SPARE
    refs, out_ref = refs[:-1], refs[-1]
    thickness = refs[0]
    if scaled == "all":
        refs = refs[1:]

    def load(f, l, t):
        span = slice(t * LANES, (t + 1) * LANES)
        x = refs[f][l, :, span]
        if scaled == "all" or f == 1:
            x = x * thickness[l, :, span]
        elif f == 2:
            closed = jnp.logical_and(last_ref[0] > 0, iota(0) == ROWS - 1)
            x = jnp.where(closed, 0.0, x)
        return x

    where = places(chunk)
    for d in range(GROUP):
        gap = (3 * d + 3) % 4
        first = d * WIDTH - 16
        a, off = (first // LANES) % TILES, first % LANES
        rel = (lane - gap * SPARE) % LANES
        sides = jnp.zeros((ROWS, LANES), jnp.float32)
        for f in range(len(chunk)):
            east, west = chunk[f]
            own = []
            for l in range(OWN):
                x = jnp.where(lane >= off, load(f, l, a), load(f, l, (a + 1) % TILES))
                at_east, at_west = where[f][l]
                sides = jnp.where(rel >= at_east, turn(x, at_east), sides)
                sides = jnp.where(rel >= at_west, turn(x, at_west - (SPARE - west)), sides)
                own.append(x)
            for i in range(3):
                out_ref[d, 3 * f + i] = jnp.where(slot == gap, turn(own[3], -SPARE * (1 + i)), own[i])
        out_ref[d, 3 * len(chunk)] = sides


def pack(chunk, scaled, last, args):
    return pl.pallas_call(
        functools.partial(pack_kernel, chunk, scaled),
        out_shape=vmem(GROUP, tile_count(chunk)),
        in_specs=[IN_SMEM] + [IN_VMEM] * len(args),
        out_specs=IN_VMEM,
        compiler_params=GRANT,
        cost_estimate=pl.CostEstimate(flops=10**6, bytes_accessed=4 << 20, transcendentals=0),
        name="pack_" + scaled,
    )(last, *(pltpu.with_memory_space_constraint(x, pltpu.HBM) for x in args))


def edges_kernel(chunk, outs, gap_ref, x_ref, *refs):
    north_ref, south_ref = refs[-2:]
    out_refs = [ref.at[k] for ref, n in zip(refs[:-2], outs) for k in range(n)]
    where = places(chunk)
    gap = gap_ref[0]
    rel = (iota(1) - gap * SPARE + LANES) % LANES
    quarter = rel // SPARE

    def group(g, _):
        for half in range(2):
            src = 2 * g + half
            sides = x_ref[src, 3 * len(chunk)]
            for f, (east, west) in enumerate(chunk):
                t = [x_ref[src, 3 * f + i] for i in range(3)]
                fourth = jnp.where(
                    quarter == 1,
                    turn(t[0], SPARE),
                    jnp.where(quarter == 2, turn(t[1], 2 * SPARE), turn(t[2], 3 * SPARE)),
                )
                for l, x in enumerate(t + [fourth]):
                    at_east, at_west = where[f][l]
                    x = jnp.where(quarter == 0, 0.0, x)
                    x = jnp.where(rel < east, turn(sides, -at_east), x)
                    in_west = jnp.logical_and(rel >= SPARE - west, rel < SPARE)
                    x = jnp.where(in_west, turn(sides, SPARE - west - at_west), x)
                    i = OWN * half + l
                    out_refs[f][OWN * src + l] = x
                    north_ref[f, g, 3 * i : 3 * i + 3, :] = x[5:8]
                    south_ref[f, g, 3 * i : 3 * i + 3, :] = x[0:3]
        return 0

    lax.fori_loop(0, 8, group, 0)


def edges(chunk, outs, gap, x):
    strip = VMEM((len(chunk), 8, 24, LANES), jnp.float32)
    return pl.pallas_call(
        functools.partial(edges_kernel, chunk, outs),
        out_shape=tuple(vmem(n, LEVELS) for n in outs) + (strip, strip),
        in_specs=[IN_SMEM, IN_VMEM],
        out_specs=(IN_VMEM,) * (len(outs) + 2),
        compiler_params=GRANT,
        name="edges",
    )(gap, *near(x))


def join_strips(north_ref, south_ref, halo_refs):
    for f, halo in enumerate(halo_refs):
        halo[...] = jnp.zeros(halo.shape, jnp.float32)

    def group(g, _):
        for f, halo in enumerate(halo_refs):
            for i in range(8):
                halo[8 * g + i, 0:3, :] = north_ref[f, g, 3 * i : 3 * i + 3, :]
                halo[8 * g + i, 5:8, :] = south_ref[f, g, 3 * i : 3 * i + 3, :]
        return 0

    lax.fori_loop(0, 8, group, 0)


def shifted(pair, by, edge):
    m, h = (pltpu.roll(x, by, 0) for x in pair)
    return jnp.where(edge, h, m), jnp.where(edge, m, h)


def coefficients(cn, ce, is_top, is_bottom):
    cs = shifted(cn, 1, is_bottom)
    out = []
    for p in range(2):
        cw = pltpu.roll(ce[p], 1, 1)
        south, west = jnp.maximum(cs[p], 0.0), jnp.maximum(cw, 0.0)
        north, east = jnp.maximum(-cn[p], 0.0), jnp.maximum(-ce[p], 0.0)
        own = 1.0 - jnp.maximum(cn[p], 0.0) + jnp.minimum(cs[p], 0.0)
        own = own - jnp.maximum(ce[p], 0.0) + jnp.minimum(cw, 0.0)
        out.append((own, north, south, east, west))
    return out


def transport(x, coefs, is_top, is_bottom, both):
    above, below = shifted(x, ROWS - 1, is_top), shifted(x, 1, is_bottom)
    out = []
    for p in range(2 if both else 1):
        own, north, south, east, west = coefs[p]
        sides = east * pltpu.roll(x[p], LANES - 1, 1) + west * pltpu.roll(x[p], 1, 1)
        out.append((own * x[p] + sides) + (north * above[p] + south * below[p]))
    return tuple(out)


def remap(count, out_ref, first_tile, prefix, final, top, inverse, h, low, high, gap):
    inverse_h = 1.0 / h
    slot = iota(1) // SPARE
    zero = jnp.zeros((ROWS, LANES), jnp.float32)

    def targets(kb, last):
        base = 1.0 + h * (8 * kb + 1).astype(jnp.float32)
        start = [prefix[f, low(kb)] for f in range(count)]

        def layers(jq, acc):
            acc = list(acc)
            for i in range(8):
                j = 8 * jq + i
                inv = inverse[j]
                u = (base - top[j]) * inv
                stride = h * inv
                values = [final[f, j] for f in range(count)]
                for k in range(8):
                    w = jnp.minimum(jnp.maximum(u, 0.0), 1.0)
                    for f in range(count):
                        acc[count * k + f] = acc[count * k + f] + w * values[f]
                    if k < 7:
                        u = u + stride
            return tuple(acc)

        acc = lax.fori_loop(low(kb), high(kb), layers, tuple(start) * 8)
        for half in range(2):
            for f in range(count):
                own = []
                for l in range(OWN):
                    k = OWN * half + l
                    below = acc[count * (k - 1) + f] if k else last[f]
                    own.append((acc[count * k + f] - below) * inverse_h)
                for i in range(3):
                    moved = turn(own[3], -SPARE * (1 + i))
                    out_ref[2 * kb + half, first_tile + 3 * f + i] = jnp.where(slot == gap, moved, own[i])
        return tuple(acc[7 * count :])

    lax.fori_loop(0, 8, targets, (zero,) * count)


def first_kernel(
    gap_ref, x_ref, c_ref, north_ref, south_ref,
    out_ref, push_ref, halo_c_ref, top, inverse, h_ref, bound_ref,
    halo_x, final, prefix, least, most,
):
    gap = gap_ref[0]
    is_top, is_bottom = iota(0) == ROWS - 1, iota(0) == 0
    join_strips(north_ref, south_ref, [halo_x.at[0], halo_x.at[1], halo_c_ref.at[0], halo_c_ref.at[1]])

    def group(g, carried):
        prefix[0, g] = carried[-1]
        least[g] = carried[-2]

        def layers(i, carried):
            runs = list(carried)
            for n in range(4):
                j = 8 * g + 4 * i + n
                mass = (x_ref[0, j], halo_x[0, j])
                theta = (x_ref[1, j], halo_x[1, j])
                coefs = coefficients((c_ref[0, j], halo_c_ref[0, j]), (c_ref[1, j], halo_c_ref[1, j]), is_top, is_bottom)
                for step in range(STEPS):
                    for p in range(2):
                        run = runs[2 * step + p]
                        middle = jnp.log(run + 0.5 * mass[p])
                        slope = pltpu.roll(middle, LANES - 1, 1) - pltpu.roll(middle, 1, 1)
                        push_ref[j, 2 * step + p] = 0.5 * theta[p] * slope
                        runs[2 * step + p] = run + mass[p]
                    both = step < STEPS - 1
                    mass = transport(mass, coefs, is_top, is_bottom, both)
                    theta = transport(theta, coefs, is_top, is_bottom, both)
                top[j] = runs[-2]
                inverse[j] = 1.0 / mass[0]
                final[0, j] = theta[0]
                runs[-2] = runs[-2] + mass[0]
                runs[-1] = runs[-1] + theta[0]
            return tuple(runs)

        return lax.fori_loop(0, 2, layers, carried)

    one, zero = jnp.ones((ROWS, LANES), jnp.float32), jnp.zeros((ROWS, LANES), jnp.float32)
    carried = lax.fori_loop(0, 8, group, (one,) * (2 * STEPS + 1) + (zero,))
    prefix[0, 8] = carried[-1]
    h = (carried[-2] - 1.0) * (1.0 / LEVELS)
    h_ref[...] = h

    inside = iota(1) // SPARE != gap
    inverse_h = 1.0 / h
    for b in range(1, 8):
        begin = (least[b] - 1.0) * inverse_h
        most[b] = jnp.max(jnp.where(inside, begin, 0.0))
        least_b = jnp.min(jnp.where(inside, begin, 1.0 * LEVELS))
        for kb in range(8):
            done = (most[b] <= 8.0 * kb + 0.99).astype(jnp.int32)
            begun = (least_b < 8.0 * kb + 8.01).astype(jnp.int32)
            bound_ref[kb] = done if b == 1 else bound_ref[kb] + done
            bound_ref[8 + kb] = 1 + begun if b == 1 else bound_ref[8 + kb] + begun

    remap(1, out_ref, 0, prefix, final, top, inverse, h, lambda kb: bound_ref[kb], lambda kb: bound_ref[8 + kb], gap)


def first_columns(gap, x, c, north, south):
    return pl.pallas_call(
        first_kernel,
        out_shape=(
            vmem(GROUP, 3),
            vmem(LEVELS, 2 * STEPS),
            vmem(2, LEVELS),
            vmem(LEVELS),
            vmem(LEVELS),
            vmem(),
            jax.ShapeDtypeStruct((16,), jnp.int32),
        ),
        in_specs=[IN_SMEM] + [IN_VMEM] * 4,
        out_specs=(IN_VMEM,) * 6 + (IN_SMEM,),
        scratch_shapes=[
            VMEM((2, LEVELS, ROWS, LANES), jnp.float32),
            VMEM((1, LEVELS, ROWS, LANES), jnp.float32),
            VMEM((1, 9, ROWS, LANES), jnp.float32),
            VMEM((8, ROWS, LANES), jnp.float32),
            SMEM((8,), jnp.float32),
        ],
        compiler_params=GRANT,
        name="first_columns",
    )(gap, *near(x, c, north, south))


def second_kernel(
    gap_ref, bound_ref, x_ref, c_ref, halo_c_ref, push_ref, north_ref, south_ref, top, inverse, h_ref, theta_ref,
    out_ref, halo, final, prefix,
):
    gap = gap_ref[0]
    is_top, is_bottom = iota(0) == ROWS - 1, iota(0) == 0
    join_strips(north_ref, south_ref, [halo.at[f] for f in range(3)])

    def group(g, carried):
        for f in range(3):
            prefix[f, g] = carried[f]

        def layers(i, carried):
            sums = list(carried)
            for n in range(4):
                j = 8 * g + 4 * i + n
                coefs = coefficients((c_ref[0, j], halo_c_ref[0, j]), (c_ref[1, j], halo_c_ref[1, j]), is_top, is_bottom)
                for f in range(3):
                    x = (x_ref[f, j], halo[f, j])
                    for step in range(STEPS):
                        if f == 0:
                            x = tuple(x[p] - push_ref[j, 2 * step + p] for p in range(2))
                        x = transport(x, coefs, is_top, is_bottom, step < STEPS - 1)
                    final[f, j] = x[0]
                    sums[f] = sums[f] + x[0]
            return tuple(sums)

        return lax.fori_loop(0, 2, layers, carried)

    zero = jnp.zeros((ROWS, LANES), jnp.float32)
    carried = lax.fori_loop(0, 8, group, (zero,) * 3)
    for f in range(3):
        prefix[f, 8] = carried[f]
    h = h_ref[...]
    remap(3, out_ref, 0, prefix, final, top, inverse, h, lambda kb: bound_ref[kb], lambda kb: bound_ref[8 + kb], gap)
    for d in range(GROUP):
        for i in range(3):
            out_ref[d, 9 + i] = theta_ref[d, i]
        out_ref[d, 12] = h


def second_columns(gap, bound, *arrays):
    return pl.pallas_call(
        second_kernel,
        out_shape=vmem(GROUP, 13),
        in_specs=[IN_SMEM] * 2 + [IN_VMEM] * len(arrays),
        out_specs=IN_VMEM,
        scratch_shapes=[
            VMEM((3, LEVELS, ROWS, LANES), jnp.float32),
            VMEM((3, LEVELS, ROWS, LANES), jnp.float32),
            VMEM((3, 9, ROWS, LANES), jnp.float32),
        ],
        compiler_params=GRANT,
        name="second_columns",
    )(gap, bound, *near(*arrays))


def unpack_kernel(x_ref, dp_ref, u_ref, v_ref, th_ref, tr_ref):
    lane = iota(1)
    slot = lane // SPARE

    def fourth(d, f):
        gap = (3 * d + 3) % 4
        t = [turn(x_ref[d, 3 * f + i], SPARE * (1 + i)) for i in range(3)]
        return jnp.where(slot == (gap + 1) % 4, t[0], jnp.where(slot == (gap + 2) % 4, t[1], t[2]))

    def merged(t, get):
        d = 4 * t // 3
        edge = (d + 1) * WIDTH - t * LANES
        return get(d) if edge >= LANES else jnp.where(lane < edge, get(d), get(d + 1))

    spans = [slice(t * LANES, (t + 1) * LANES) for t in range(TILES)]
    for t, span in enumerate(spans):
        h = merged(t, lambda d: x_ref[d, 12])
        for l in range(OWN):
            dp_ref[l, :, span] = h
    for f, ref in enumerate((u_ref, v_ref, tr_ref, th_ref)):
        last = [fourth(d, f) for d in range(GROUP)]
        for t, span in enumerate(spans):
            for l in range(3):
                ref[l, :, span] = merged(t, lambda d: x_ref[d, 3 * f + l])
            ref[3, :, span] = merged(t, lambda d: last[d])


def unpack(x):
    shape = jax.ShapeDtypeStruct((OWN, ROWS, TILES * LANES), jnp.float32)
    return pl.pallas_call(
        unpack_kernel,
        out_shape=(shape,) * 5,
        in_specs=[IN_VMEM],
        out_specs=(IN_VMEM,) * 5,
        compiler_params=GRANT,
        name="unpack",
    )(*near(x))


def body(dp, u, v, th, tr, cn, ce):
    lats = lax.axis_size("lat")
    last = (lax.axis_index("lat") == lats - 1).astype(jnp.int32).reshape(1)
    gap = ((3 * lax.axis_index("lev") + 3) % 4).astype(jnp.int32).reshape(1)
    forward = [(i, (i + 1) % lats) for i in range(lats)]
    backward = [(b, a) for a, b in forward]

    def across(x):
        return lax.all_to_all(x, "lev", 0, 0, tiled=True)

    def strips(to_north, to_south):
        return lax.ppermute(to_south, "lat", backward), lax.ppermute(to_north, "lat", forward)

    held_a = across(pack(CHUNK_A, "one", last, (dp, th, cn, ce)))
    sent_b = pack(CHUNK_B, "all", last, (dp, u, v, tr))
    x_a, courant, to_north, to_south = edges(CHUNK_A, (2, 2), gap, held_a)

    north_a, south_a = strips(to_north, to_south)
    x_b, to_north, to_south = edges(CHUNK_B, (3,), gap, across(sent_b))
    north_b, south_b = strips(to_north, to_south)
    theta, push, halo_c, top, inverse, h, bound = first_columns(gap, x_a, courant, north_a, south_a)
    made = second_columns(gap, bound, x_b, courant, halo_c, push, north_b, south_b, top, inverse, h, theta)
    return tuple(unpack(across(made)))


def solution(mesh):
    spec = P("lev", "lat", None)
    return jax.shard_map(body, mesh=mesh, in_specs=(spec,) * 7, out_specs=(spec,) * 5, check_vma=False)
```

```python
import functools

import jax
import jax.numpy as jnp
from jax import lax
from jax.experimental import pallas as pl
from jax.experimental.pallas import tpu as pltpu
from jax.sharding import PartitionSpec as P

STEPS = 3
LEVELS = 64
OWN = 4
GROUP = 16
WIDTH = 96
SPARE = 32
LANES = 128
TILES = 12
ROWS = 8
VMEM, SMEM = pltpu.VMEM, pltpu.SMEM

CHUNK_A = ((4, 4), (3, 3), (3, 3), (3, 4))
CHUNK_B = ((3, 3), (3, 3), (3, 3))


def places(chunk):
    at, out = 0, []
    for east, west in chunk:
        out.append([])
        for _ in range(OWN):
            out[-1].append((at, at + east))
            at += east + west
    assert at <= LANES
    return out


def tile_count(chunk):
    return 3 * len(chunk) + 1


def turn(x, by):
    by %= LANES
    return pltpu.roll(x, by, 1) if by else x


def iota(axis):
    return lax.broadcasted_iota(jnp.int32, (ROWS, LANES), axis)


def vmem(*shape):
    return VMEM(shape + (ROWS, LANES), jnp.float32)


IN_VMEM = pl.BlockSpec(memory_space=VMEM)
IN_SMEM = pl.BlockSpec(memory_space=SMEM)
GRANT = pltpu.CompilerParams(vmem_limit_bytes=16 << 20)


def near(*arrays):
    return tuple(pltpu.with_memory_space_constraint(x, VMEM) for x in arrays)


def pack_kernel(chunk, scaled, last_ref, *refs):
    lane = iota(1)
    slot = lane // SPARE
    refs, out_ref = refs[:-1], refs[-1]
    thickness = refs[0]
    if scaled == "all":
        refs = refs[1:]

    def load(f, l, t):
        span = slice(t * LANES, (t + 1) * LANES)
        x = refs[f][l, :, span]
        if scaled == "all" or f == 1:
            x = x * thickness[l, :, span]
        elif f == 2:
            closed = jnp.logical_and(last_ref[0] > 0, iota(0) == ROWS - 1)
            x = jnp.where(closed, 0.0, x)
        return x

    where = places(chunk)
    for d in range(GROUP):
        gap = (3 * d + 3) % 4
        first = d * WIDTH - 16
        a, off = (first // LANES) % TILES, first % LANES
        rel = (lane - gap * SPARE) % LANES
        sides = jnp.zeros((ROWS, LANES), jnp.float32)
        for f in range(len(chunk)):
            east, west = chunk[f]
            own = []
            for l in range(OWN):
                x = jnp.where(lane >= off, load(f, l, a), load(f, l, (a + 1) % TILES))
                at_east, at_west = where[f][l]
                sides = jnp.where(rel >= at_east, turn(x, at_east), sides)
                sides = jnp.where(rel >= at_west, turn(x, at_west - (SPARE - west)), sides)
                own.append(x)
            for i in range(3):
                out_ref[d, 3 * f + i] = jnp.where(slot == gap, turn(own[3], -SPARE * (1 + i)), own[i])
        out_ref[d, 3 * len(chunk)] = sides


def pack(chunk, scaled, last, args):
    return pl.pallas_call(
        functools.partial(pack_kernel, chunk, scaled),
        out_shape=vmem(GROUP, tile_count(chunk)),
        in_specs=[IN_SMEM] + [IN_VMEM] * len(args),
        out_specs=IN_VMEM,
        compiler_params=GRANT,
        cost_estimate=pl.CostEstimate(flops=10**6, bytes_accessed=4 << 20, transcendentals=0),
        name="pack_" + scaled,
    )(last, *(pltpu.with_memory_space_constraint(x, pltpu.HBM) for x in args))


def edges_kernel(chunk, outs, gap_ref, x_ref, *refs):
    first_ref, second_ref = refs[-2:]
    even = gap_ref[1] > 0
    out_refs = [ref.at[k] for ref, n in zip(refs[:-2], outs) for k in range(n)]
    where = places(chunk)
    gap = gap_ref[0]
    rel = (iota(1) - gap * SPARE + LANES) % LANES
    quarter = rel // SPARE

    def group(g, _):
        for half in range(2):
            src = 2 * g + half
            sides = x_ref[src, 3 * len(chunk)]
            for f, (east, west) in enumerate(chunk):
                t = [x_ref[src, 3 * f + i] for i in range(3)]
                fourth = jnp.where(
                    quarter == 1,
                    turn(t[0], SPARE),
                    jnp.where(quarter == 2, turn(t[1], 2 * SPARE), turn(t[2], 3 * SPARE)),
                )
                for l, x in enumerate(t + [fourth]):
                    at_east, at_west = where[f][l]
                    x = jnp.where(quarter == 0, 0.0, x)
                    x = jnp.where(rel < east, turn(sides, -at_east), x)
                    in_west = jnp.logical_and(rel >= SPARE - west, rel < SPARE)
                    x = jnp.where(in_west, turn(sides, SPARE - west - at_west), x)
                    i = OWN * half + l
                    out_refs[f][OWN * src + l] = x
                    north = pltpu.roll(x, 3, 0)
                    first_ref[f, g, 3 * i : 3 * i + 3, :] = jnp.where(even, north, x)[0:3]
                    second_ref[f, g, 3 * i : 3 * i + 3, :] = jnp.where(even, x, north)[0:3]
        return 0

    lax.fori_loop(0, 8, group, 0)


def edges(chunk, outs, gap, x):
    strip = VMEM((len(chunk), 8, 24, LANES), jnp.float32)
    return pl.pallas_call(
        functools.partial(edges_kernel, chunk, outs),
        out_shape=tuple(vmem(n, LEVELS) for n in outs) + (strip, strip),
        in_specs=[IN_SMEM, IN_VMEM],
        out_specs=(IN_VMEM,) * (len(outs) + 2),
        compiler_params=GRANT,
        name="edges",
    )(gap, *near(x))


def join_strips(even, first_ref, second_ref, halo_refs):
    for f, halo in enumerate(halo_refs):
        halo[...] = jnp.zeros(halo.shape, jnp.float32)

    def group(g, _):
        for f, halo in enumerate(halo_refs):
            for i in range(8):
                a, b = (ref[f, g, 3 * i : 3 * i + 3, :] for ref in (first_ref, second_ref))
                halo[8 * g + i, 0:3, :] = jnp.where(even, a, b)
                halo[8 * g + i, 5:8, :] = jnp.where(even, b, a)
        return 0

    lax.fori_loop(0, 8, group, 0)


def shifted(pair, by, edge):
    m, h = (pltpu.roll(x, by, 0) for x in pair)
    return jnp.where(edge, h, m), jnp.where(edge, m, h)


def coefficients(cn, ce, is_top, is_bottom):
    cs = shifted(cn, 1, is_bottom)
    out = []
    for p in range(2):
        cw = pltpu.roll(ce[p], 1, 1)
        south, west = jnp.maximum(cs[p], 0.0), jnp.maximum(cw, 0.0)
        north, east = jnp.maximum(-cn[p], 0.0), jnp.maximum(-ce[p], 0.0)
        own = 1.0 - jnp.maximum(cn[p], 0.0) + jnp.minimum(cs[p], 0.0)
        own = own - jnp.maximum(ce[p], 0.0) + jnp.minimum(cw, 0.0)
        out.append((own, north, south, east, west))
    return out


def transport(x, coefs, is_top, is_bottom, both):
    above, below = shifted(x, ROWS - 1, is_top), shifted(x, 1, is_bottom)
    out = []
    for p in range(2 if both else 1):
        own, north, south, east, west = coefs[p]
        sides = east * pltpu.roll(x[p], LANES - 1, 1) + west * pltpu.roll(x[p], 1, 1)
        out.append((own * x[p] + sides) + (north * above[p] + south * below[p]))
    return tuple(out)


def remap(count, out_ref, first_tile, prefix, final, top, inverse, h, low, high, gap):
    inverse_h = 1.0 / h
    slot = iota(1) // SPARE
    zero = jnp.zeros((ROWS, LANES), jnp.float32)

    def targets(kb, last):
        base = 1.0 + h * (8 * kb + 1).astype(jnp.float32)
        start = [prefix[f, low(kb)] for f in range(count)]

        def layers(jq, acc):
            acc = list(acc)
            for i in range(8):
                j = 8 * jq + i
                inv = inverse[j]
                u = (base - top[j]) * inv
                stride = h * inv
                values = [final[f, j] for f in range(count)]
                for k in range(8):
                    w = jnp.minimum(jnp.maximum(u, 0.0), 1.0)
                    for f in range(count):
                        acc[count * k + f] = acc[count * k + f] + w * values[f]
                    if k < 7:
                        u = u + stride
            return tuple(acc)

        acc = lax.fori_loop(low(kb), high(kb), layers, tuple(start) * 8)
        for half in range(2):
            for f in range(count):
                own = []
                for l in range(OWN):
                    k = OWN * half + l
                    below = acc[count * (k - 1) + f] if k else last[f]
                    own.append((acc[count * k + f] - below) * inverse_h)
                for i in range(3):
                    moved = turn(own[3], -SPARE * (1 + i))
                    out_ref[2 * kb + half, first_tile + 3 * f + i] = jnp.where(slot == gap, moved, own[i])
        return tuple(acc[7 * count :])

    lax.fori_loop(0, 8, targets, (zero,) * count)


def first_kernel(
    gap_ref, x_ref, c_ref, first_ref, second_ref,
    out_ref, push_ref, halo_c_ref, top, inverse, h_ref, bound_ref,
    halo_x, final, prefix, least, most,
):
    gap = gap_ref[0]
    is_top, is_bottom = iota(0) == ROWS - 1, iota(0) == 0
    join_strips(gap_ref[1] > 0, first_ref, second_ref, [halo_x.at[0], halo_x.at[1], halo_c_ref.at[0], halo_c_ref.at[1]])

    def group(g, carried):
        prefix[0, g] = carried[-1]
        least[g] = carried[-2]

        def layers(i, carried):
            runs = list(carried)
            for n in range(4):
                j = 8 * g + 4 * i + n
                mass = (x_ref[0, j], halo_x[0, j])
                theta = (x_ref[1, j], halo_x[1, j])
                coefs = coefficients((c_ref[0, j], halo_c_ref[0, j]), (c_ref[1, j], halo_c_ref[1, j]), is_top, is_bottom)
                for step in range(STEPS):
                    for p in range(2):
                        run = runs[2 * step + p]
                        middle = jnp.log(run + 0.5 * mass[p])
                        slope = pltpu.roll(middle, LANES - 1, 1) - pltpu.roll(middle, 1, 1)
                        push_ref[j, 2 * step + p] = 0.5 * theta[p] * slope
                        runs[2 * step + p] = run + mass[p]
                    both = step < STEPS - 1
                    mass = transport(mass, coefs, is_top, is_bottom, both)
                    theta = transport(theta, coefs, is_top, is_bottom, both)
                top[j] = runs[-2]
                inverse[j] = 1.0 / mass[0]
                final[0, j] = theta[0]
                runs[-2] = runs[-2] + mass[0]
                runs[-1] = runs[-1] + theta[0]
            return tuple(runs)

        return lax.fori_loop(0, 2, layers, carried)

    one, zero = jnp.ones((ROWS, LANES), jnp.float32), jnp.zeros((ROWS, LANES), jnp.float32)
    carried = lax.fori_loop(0, 8, group, (one,) * (2 * STEPS + 1) + (zero,))
    prefix[0, 8] = carried[-1]
    h = (carried[-2] - 1.0) * (1.0 / LEVELS)
    h_ref[...] = h

    inside = iota(1) // SPARE != gap
    inverse_h = 1.0 / h
    for b in range(1, 8):
        begin = (least[b] - 1.0) * inverse_h
        most[b] = jnp.max(jnp.where(inside, begin, 0.0))
        least_b = jnp.min(jnp.where(inside, begin, 1.0 * LEVELS))
        for kb in range(8):
            done = (most[b] <= 8.0 * kb + 0.99).astype(jnp.int32)
            begun = (least_b < 8.0 * kb + 8.01).astype(jnp.int32)
            bound_ref[kb] = done if b == 1 else bound_ref[kb] + done
            bound_ref[8 + kb] = 1 + begun if b == 1 else bound_ref[8 + kb] + begun

    remap(1, out_ref, 0, prefix, final, top, inverse, h, lambda kb: bound_ref[kb], lambda kb: bound_ref[8 + kb], gap)


def first_columns(gap, x, c, north, south):
    return pl.pallas_call(
        first_kernel,
        out_shape=(
            vmem(GROUP, 3),
            vmem(LEVELS, 2 * STEPS),
            vmem(2, LEVELS),
            vmem(LEVELS),
            vmem(LEVELS),
            vmem(),
            jax.ShapeDtypeStruct((16,), jnp.int32),
        ),
        in_specs=[IN_SMEM] + [IN_VMEM] * 4,
        out_specs=(IN_VMEM,) * 6 + (IN_SMEM,),
        scratch_shapes=[
            VMEM((2, LEVELS, ROWS, LANES), jnp.float32),
            VMEM((1, LEVELS, ROWS, LANES), jnp.float32),
            VMEM((1, 9, ROWS, LANES), jnp.float32),
            VMEM((8, ROWS, LANES), jnp.float32),
            SMEM((8,), jnp.float32),
        ],
        compiler_params=GRANT,
        name="first_columns",
    )(gap, *near(x, c, north, south))


def second_kernel(
    gap_ref, bound_ref, x_ref, c_ref, halo_c_ref, push_ref, first_ref, second_ref, top, inverse, h_ref, theta_ref,
    out_ref, halo, final, prefix,
):
    gap = gap_ref[0]
    is_top, is_bottom = iota(0) == ROWS - 1, iota(0) == 0
    join_strips(gap_ref[1] > 0, first_ref, second_ref, [halo.at[f] for f in range(3)])

    def group(g, carried):
        for f in range(3):
            prefix[f, g] = carried[f]

        def layers(i, carried):
            sums = list(carried)
            for n in range(4):
                j = 8 * g + 4 * i + n
                coefs = coefficients((c_ref[0, j], halo_c_ref[0, j]), (c_ref[1, j], halo_c_ref[1, j]), is_top, is_bottom)
                for f in range(3):
                    x = (x_ref[f, j], halo[f, j])
                    for step in range(STEPS):
                        if f == 0:
                            x = tuple(x[p] - push_ref[j, 2 * step + p] for p in range(2))
                        x = transport(x, coefs, is_top, is_bottom, step < STEPS - 1)
                    final[f, j] = x[0]
                    sums[f] = sums[f] + x[0]
            return tuple(sums)

        return lax.fori_loop(0, 2, layers, carried)

    zero = jnp.zeros((ROWS, LANES), jnp.float32)
    carried = lax.fori_loop(0, 8, group, (zero,) * 3)
    for f in range(3):
        prefix[f, 8] = carried[f]
    h = h_ref[...]
    remap(3, out_ref, 0, prefix, final, top, inverse, h, lambda kb: bound_ref[kb], lambda kb: bound_ref[8 + kb], gap)
    for d in range(GROUP):
        for i in range(3):
            out_ref[d, 9 + i] = theta_ref[d, i]
        out_ref[d, 12] = h


def second_columns(gap, bound, *arrays):
    return pl.pallas_call(
        second_kernel,
        out_shape=vmem(GROUP, 13),
        in_specs=[IN_SMEM] * 2 + [IN_VMEM] * len(arrays),
        out_specs=IN_VMEM,
        scratch_shapes=[
            VMEM((3, LEVELS, ROWS, LANES), jnp.float32),
            VMEM((3, LEVELS, ROWS, LANES), jnp.float32),
            VMEM((3, 9, ROWS, LANES), jnp.float32),
        ],
        compiler_params=GRANT,
        name="second_columns",
    )(gap, bound, *near(*arrays))


def unpack_kernel(x_ref, dp_ref, u_ref, v_ref, th_ref, tr_ref):
    lane = iota(1)
    slot = lane // SPARE

    def fourth(d, f):
        gap = (3 * d + 3) % 4
        t = [turn(x_ref[d, 3 * f + i], SPARE * (1 + i)) for i in range(3)]
        return jnp.where(slot == (gap + 1) % 4, t[0], jnp.where(slot == (gap + 2) % 4, t[1], t[2]))

    def merged(t, get):
        d = 4 * t // 3
        edge = (d + 1) * WIDTH - t * LANES
        return get(d) if edge >= LANES else jnp.where(lane < edge, get(d), get(d + 1))

    spans = [slice(t * LANES, (t + 1) * LANES) for t in range(TILES)]
    for t, span in enumerate(spans):
        h = merged(t, lambda d: x_ref[d, 12])
        for l in range(OWN):
            dp_ref[l, :, span] = h
    for f, ref in enumerate((u_ref, v_ref, tr_ref, th_ref)):
        last = [fourth(d, f) for d in range(GROUP)]
        for t, span in enumerate(spans):
            for l in range(3):
                ref[l, :, span] = merged(t, lambda d: x_ref[d, 3 * f + l])
            ref[3, :, span] = merged(t, lambda d: last[d])


def unpack(x):
    shape = jax.ShapeDtypeStruct((OWN, ROWS, TILES * LANES), jnp.float32)
    return pl.pallas_call(
        unpack_kernel,
        out_shape=(shape,) * 5,
        in_specs=[IN_VMEM],
        out_specs=(IN_VMEM,) * 5,
        compiler_params=GRANT,
        name="unpack",
    )(*near(x))


def body(dp, u, v, th, tr, cn, ce):
    lats = lax.axis_size("lat")
    last = (lax.axis_index("lat") == lats - 1).astype(jnp.int32).reshape(1)
    gap = jnp.stack([(3 * lax.axis_index("lev") + 3) % 4, 1 - lax.axis_index("lat") % 2]).astype(jnp.int32)
    swaps = [[(i, i + 1) for i in range(start, lats - 1, 2)] for start in (0, 1)]
    swaps = [pairs + [(b, a) for a, b in pairs] for pairs in swaps]

    def across(x):
        return lax.all_to_all(x, "lev", 0, 0, tiled=True)

    def strips(first, second):
        return lax.ppermute(first, "lat", swaps[0]), lax.ppermute(second, "lat", swaps[1])

    held_a = across(pack(CHUNK_A, "one", last, (dp, th, cn, ce)))
    sent_b = pack(CHUNK_B, "all", last, (dp, u, v, tr))
    x_a, courant, first, second = edges(CHUNK_A, (2, 2), gap, held_a)

    first_a, second_a = strips(first, second)
    x_b, first, second = edges(CHUNK_B, (3,), gap, across(sent_b))
    first_b, second_b = strips(first, second)
    theta, push, halo_c, top, inverse, h, bound = first_columns(gap, x_a, courant, first_a, second_a)
    made = second_columns(gap, bound, x_b, courant, halo_c, push, first_b, second_b, top, inverse, h, theta)
    return tuple(unpack(across(made)))


def solution(mesh):
    spec = P("lev", "lat", None)
    return jax.shard_map(body, mesh=mesh, in_specs=(spec,) * 7, out_specs=(spec,) * 5, check_vma=False)
```

```python
import functools

import jax
import jax.numpy as jnp
from jax import lax
from jax.experimental import pallas as pl
from jax.experimental.pallas import tpu as pltpu
from jax.sharding import PartitionSpec as P

STEPS = 3
LEVELS = 64
OWN = 4
GROUP = 16
WIDTH = 96
SPARE = 32
LANES = 128
TILES = 12
ROWS = 8
VMEM, SMEM = pltpu.VMEM, pltpu.SMEM

CHUNK_A = ((4, 4), (3, 3), (3, 3), (3, 4))
CHUNK_B = ((3, 3), (3, 3), (3, 3))


def places(chunk):
    at, out = 0, []
    for east, west in chunk:
        out.append([])
        for _ in range(OWN):
            out[-1].append((at, at + east))
            at += east + west
    assert at <= LANES
    return out


def tile_count(chunk):
    return 3 * len(chunk) + 1


def turn(x, by):
    by %= LANES
    return pltpu.roll(x, by, 1) if by else x


def iota(axis):
    return lax.broadcasted_iota(jnp.int32, (ROWS, LANES), axis)


def vmem(*shape):
    return VMEM(shape + (ROWS, LANES), jnp.float32)


IN_VMEM = pl.BlockSpec(memory_space=VMEM)
IN_SMEM = pl.BlockSpec(memory_space=SMEM)
GRANT = pltpu.CompilerParams(vmem_limit_bytes=16 << 20)


def near(*arrays):
    return tuple(pltpu.with_memory_space_constraint(x, VMEM) for x in arrays)


def pack_kernel(chunk, scaled, last_ref, *refs):
    lane = iota(1)
    slot = lane // SPARE
    refs, out_ref = refs[:-1], refs[-1]
    thickness = refs[0]
    if scaled == "all":
        refs = refs[1:]

    def load(f, l, t):
        span = slice(t * LANES, (t + 1) * LANES)
        x = refs[f][l, :, span]
        if scaled == "all" or f == 1:
            x = x * thickness[l, :, span]
        elif f == 2:
            closed = jnp.logical_and(last_ref[0] > 0, iota(0) == ROWS - 1)
            x = jnp.where(closed, 0.0, x)
        return x

    where = places(chunk)
    for d in range(GROUP):
        gap = (3 * d + 3) % 4
        first = d * WIDTH - 16
        a, off = (first // LANES) % TILES, first % LANES
        rel = (lane - gap * SPARE) % LANES
        sides = jnp.zeros((ROWS, LANES), jnp.float32)
        for f in range(len(chunk)):
            east, west = chunk[f]
            own = []
            for l in range(OWN):
                x = jnp.where(lane >= off, load(f, l, a), load(f, l, (a + 1) % TILES))
                at_east, at_west = where[f][l]
                sides = jnp.where(rel >= at_east, turn(x, at_east), sides)
                sides = jnp.where(rel >= at_west, turn(x, at_west - (SPARE - west)), sides)
                own.append(x)
            for i in range(3):
                out_ref[d, 3 * f + i] = jnp.where(slot == gap, turn(own[3], -SPARE * (1 + i)), own[i])
        out_ref[d, 3 * len(chunk)] = sides


def pack(chunk, scaled, last, args):
    return pl.pallas_call(
        functools.partial(pack_kernel, chunk, scaled),
        out_shape=vmem(GROUP, tile_count(chunk)),
        in_specs=[IN_SMEM] + [IN_VMEM] * len(args),
        out_specs=IN_VMEM,
        compiler_params=GRANT,
        cost_estimate=pl.CostEstimate(flops=10**6, bytes_accessed=4 << 20, transcendentals=0),
        name="pack_" + scaled,
    )(last, *(pltpu.with_memory_space_constraint(x, pltpu.HBM) for x in args))


def in_order(even, act, refs):
    first_ref, second_ref = refs[-2:]

    @pl.when(even)
    def _():
        act(first_ref, second_ref)

    @pl.when(jnp.logical_not(even))
    def _():
        act(second_ref, first_ref)


def edges_kernel(chunk, outs, gap_ref, x_ref, *refs):
    out_refs = [ref.at[k] for ref, n in zip(refs[:-2], outs) for k in range(n)]
    where = places(chunk)
    gap = gap_ref[0] % 4
    rel = (iota(1) - gap * SPARE + LANES) % LANES
    quarter = rel // SPARE

    def group(north_ref, south_ref, g, _):
        for half in range(2):
            src = 2 * g + half
            sides = x_ref[src, 3 * len(chunk)]
            for f, (east, west) in enumerate(chunk):
                t = [x_ref[src, 3 * f + i] for i in range(3)]
                fourth = jnp.where(
                    quarter == 1,
                    turn(t[0], SPARE),
                    jnp.where(quarter == 2, turn(t[1], 2 * SPARE), turn(t[2], 3 * SPARE)),
                )
                for l, x in enumerate(t + [fourth]):
                    at_east, at_west = where[f][l]
                    x = jnp.where(quarter == 0, 0.0, x)
                    x = jnp.where(rel < east, turn(sides, -at_east), x)
                    in_west = jnp.logical_and(rel >= SPARE - west, rel < SPARE)
                    x = jnp.where(in_west, turn(sides, SPARE - west - at_west), x)
                    i = OWN * half + l
                    out_refs[f][OWN * src + l] = x
                    north_ref[f, g, 3 * i : 3 * i + 3, :] = x[5:8]
                    south_ref[f, g, 3 * i : 3 * i + 3, :] = x[0:3]
        return 0

    in_order(gap_ref[0] >= 4, lambda north, south: lax.fori_loop(0, 8, functools.partial(group, north, south), 0), refs)


def edges(chunk, outs, gap, x):
    strip = VMEM((len(chunk), 8, 24, LANES), jnp.float32)
    return pl.pallas_call(
        functools.partial(edges_kernel, chunk, outs),
        out_shape=tuple(vmem(n, LEVELS) for n in outs) + (strip, strip),
        in_specs=[IN_SMEM, IN_VMEM],
        out_specs=(IN_VMEM,) * (len(outs) + 2),
        compiler_params=GRANT,
        name="edges",
    )(gap, *near(x))


def join_strips(even, first_ref, second_ref, halo_refs):
    for f, halo in enumerate(halo_refs):
        halo[...] = jnp.zeros(halo.shape, jnp.float32)

    def group(north_ref, south_ref, g, _):
        for f, halo in enumerate(halo_refs):
            for i in range(8):
                halo[8 * g + i, 0:3, :] = north_ref[f, g, 3 * i : 3 * i + 3, :]
                halo[8 * g + i, 5:8, :] = south_ref[f, g, 3 * i : 3 * i + 3, :]
        return 0

    act = lambda north, south: lax.fori_loop(0, 8, functools.partial(group, north, south), 0)
    in_order(even, act, (first_ref, second_ref))


def shifted(pair, by, edge):
    m, h = (pltpu.roll(x, by, 0) for x in pair)
    return jnp.where(edge, h, m), jnp.where(edge, m, h)


def coefficients(cn, ce, is_top, is_bottom):
    cs = shifted(cn, 1, is_bottom)
    out = []
    for p in range(2):
        cw = pltpu.roll(ce[p], 1, 1)
        south, west = jnp.maximum(cs[p], 0.0), jnp.maximum(cw, 0.0)
        north, east = jnp.maximum(-cn[p], 0.0), jnp.maximum(-ce[p], 0.0)
        own = 1.0 - jnp.maximum(cn[p], 0.0) + jnp.minimum(cs[p], 0.0)
        own = own - jnp.maximum(ce[p], 0.0) + jnp.minimum(cw, 0.0)
        out.append((own, north, south, east, west))
    return out


def transport(x, coefs, is_top, is_bottom, both):
    above, below = shifted(x, ROWS - 1, is_top), shifted(x, 1, is_bottom)
    out = []
    for p in range(2 if both else 1):
        own, north, south, east, west = coefs[p]
        sides = east * pltpu.roll(x[p], LANES - 1, 1) + west * pltpu.roll(x[p], 1, 1)
        out.append((own * x[p] + sides) + (north * above[p] + south * below[p]))
    return tuple(out)


def remap(count, out_ref, first_tile, prefix, final, top, inverse, h, low, high, gap):
    inverse_h = 1.0 / h
    slot = iota(1) // SPARE
    zero = jnp.zeros((ROWS, LANES), jnp.float32)

    def targets(kb, last):
        base = 1.0 + h * (8 * kb + 1).astype(jnp.float32)
        start = [prefix[f, low(kb)] for f in range(count)]

        def layers(jq, acc):
            acc = list(acc)
            for i in range(8):
                j = 8 * jq + i
                inv = inverse[j]
                u = (base - top[j]) * inv
                stride = h * inv
                values = [final[f, j] for f in range(count)]
                for k in range(8):
                    w = jnp.minimum(jnp.maximum(u, 0.0), 1.0)
                    for f in range(count):
                        acc[count * k + f] = acc[count * k + f] + w * values[f]
                    if k < 7:
                        u = u + stride
            return tuple(acc)

        acc = lax.fori_loop(low(kb), high(kb), layers, tuple(start) * 8)
        for half in range(2):
            for f in range(count):
                own = []
                for l in range(OWN):
                    k = OWN * half + l
                    below = acc[count * (k - 1) + f] if k else last[f]
                    own.append((acc[count * k + f] - below) * inverse_h)
                for i in range(3):
                    moved = turn(own[3], -SPARE * (1 + i))
                    out_ref[2 * kb + half, first_tile + 3 * f + i] = jnp.where(slot == gap, moved, own[i])
        return tuple(acc[7 * count :])

    lax.fori_loop(0, 8, targets, (zero,) * count)


def first_kernel(
    gap_ref, x_ref, c_ref, first_ref, second_ref,
    out_ref, push_ref, halo_c_ref, top, inverse, h_ref, bound_ref,
    halo_x, final, prefix, least, most,
):
    gap = gap_ref[0] % 4
    is_top, is_bottom = iota(0) == ROWS - 1, iota(0) == 0
    join_strips(gap_ref[0] >= 4, first_ref, second_ref, [halo_x.at[0], halo_x.at[1], halo_c_ref.at[0], halo_c_ref.at[1]])

    def group(g, carried):
        prefix[0, g] = carried[-1]
        least[g] = carried[-2]

        def layers(i, carried):
            runs = list(carried)
            for n in range(4):
                j = 8 * g + 4 * i + n
                mass = (x_ref[0, j], halo_x[0, j])
                theta = (x_ref[1, j], halo_x[1, j])
                coefs = coefficients((c_ref[0, j], halo_c_ref[0, j]), (c_ref[1, j], halo_c_ref[1, j]), is_top, is_bottom)
                for step in range(STEPS):
                    for p in range(2):
                        run = runs[2 * step + p]
                        middle = jnp.log(run + 0.5 * mass[p])
                        slope = pltpu.roll(middle, LANES - 1, 1) - pltpu.roll(middle, 1, 1)
                        push_ref[j, 2 * step + p] = 0.5 * theta[p] * slope
                        runs[2 * step + p] = run + mass[p]
                    both = step < STEPS - 1
                    mass = transport(mass, coefs, is_top, is_bottom, both)
                    theta = transport(theta, coefs, is_top, is_bottom, both)
                top[j] = runs[-2]
                inverse[j] = 1.0 / mass[0]
                final[0, j] = theta[0]
                runs[-2] = runs[-2] + mass[0]
                runs[-1] = runs[-1] + theta[0]
            return tuple(runs)

        return lax.fori_loop(0, 2, layers, carried)

    one, zero = jnp.ones((ROWS, LANES), jnp.float32), jnp.zeros((ROWS, LANES), jnp.float32)
    carried = lax.fori_loop(0, 8, group, (one,) * (2 * STEPS + 1) + (zero,))
    prefix[0, 8] = carried[-1]
    h = (carried[-2] - 1.0) * (1.0 / LEVELS)
    h_ref[...] = h

    inside = iota(1) // SPARE != gap
    inverse_h = 1.0 / h
    for b in range(1, 8):
        begin = (least[b] - 1.0) * inverse_h
        most[b] = jnp.max(jnp.where(inside, begin, 0.0))
        least_b = jnp.min(jnp.where(inside, begin, 1.0 * LEVELS))
        for kb in range(8):
            done = (most[b] <= 8.0 * kb + 0.99).astype(jnp.int32)
            begun = (least_b < 8.0 * kb + 8.01).astype(jnp.int32)
            bound_ref[kb] = done if b == 1 else bound_ref[kb] + done
            bound_ref[8 + kb] = 1 + begun if b == 1 else bound_ref[8 + kb] + begun

    remap(1, out_ref, 0, prefix, final, top, inverse, h, lambda kb: bound_ref[kb], lambda kb: bound_ref[8 + kb], gap)


def first_columns(gap, x, c, north, south):
    return pl.pallas_call(
        first_kernel,
        out_shape=(
            vmem(GROUP, 3),
            vmem(LEVELS, 2 * STEPS),
            vmem(2, LEVELS),
            vmem(LEVELS),
            vmem(LEVELS),
            vmem(),
            jax.ShapeDtypeStruct((16,), jnp.int32),
        ),
        in_specs=[IN_SMEM] + [IN_VMEM] * 4,
        out_specs=(IN_VMEM,) * 6 + (IN_SMEM,),
        scratch_shapes=[
            VMEM((2, LEVELS, ROWS, LANES), jnp.float32),
            VMEM((1, LEVELS, ROWS, LANES), jnp.float32),
            VMEM((1, 9, ROWS, LANES), jnp.float32),
            VMEM((8, ROWS, LANES), jnp.float32),
            SMEM((8,), jnp.float32),
        ],
        compiler_params=GRANT,
        name="first_columns",
    )(gap, *near(x, c, north, south))


def second_kernel(
    gap_ref, bound_ref, x_ref, c_ref, halo_c_ref, push_ref, first_ref, second_ref, top, inverse, h_ref, theta_ref,
    out_ref, halo, final, prefix,
):
    gap = gap_ref[0] % 4
    is_top, is_bottom = iota(0) == ROWS - 1, iota(0) == 0
    join_strips(gap_ref[0] >= 4, first_ref, second_ref, [halo.at[f] for f in range(3)])

    def group(g, carried):
        for f in range(3):
            prefix[f, g] = carried[f]

        def layers(i, carried):
            sums = list(carried)
            for n in range(4):
                j = 8 * g + 4 * i + n
                coefs = coefficients((c_ref[0, j], halo_c_ref[0, j]), (c_ref[1, j], halo_c_ref[1, j]), is_top, is_bottom)
                for f in range(3):
                    x = (x_ref[f, j], halo[f, j])
                    for step in range(STEPS):
                        if f == 0:
                            x = tuple(x[p] - push_ref[j, 2 * step + p] for p in range(2))
                        x = transport(x, coefs, is_top, is_bottom, step < STEPS - 1)
                    final[f, j] = x[0]
                    sums[f] = sums[f] + x[0]
            return tuple(sums)

        return lax.fori_loop(0, 2, layers, carried)

    zero = jnp.zeros((ROWS, LANES), jnp.float32)
    carried = lax.fori_loop(0, 8, group, (zero,) * 3)
    for f in range(3):
        prefix[f, 8] = carried[f]
    h = h_ref[...]
    remap(3, out_ref, 0, prefix, final, top, inverse, h, lambda kb: bound_ref[kb], lambda kb: bound_ref[8 + kb], gap)
    for d in range(GROUP):
        for i in range(3):
            out_ref[d, 9 + i] = theta_ref[d, i]
        out_ref[d, 12] = h


def second_columns(gap, bound, *arrays):
    return pl.pallas_call(
        second_kernel,
        out_shape=vmem(GROUP, 13),
        in_specs=[IN_SMEM] * 2 + [IN_VMEM] * len(arrays),
        out_specs=IN_VMEM,
        scratch_shapes=[
            VMEM((3, LEVELS, ROWS, LANES), jnp.float32),
            VMEM((3, LEVELS, ROWS, LANES), jnp.float32),
            VMEM((3, 9, ROWS, LANES), jnp.float32),
        ],
        compiler_params=GRANT,
        name="second_columns",
    )(gap, bound, *near(*arrays))


def unpack_kernel(x_ref, dp_ref, u_ref, v_ref, th_ref, tr_ref):
    lane = iota(1)
    slot = lane // SPARE

    def fourth(d, f):
        gap = (3 * d + 3) % 4
        t = [turn(x_ref[d, 3 * f + i], SPARE * (1 + i)) for i in range(3)]
        return jnp.where(slot == (gap + 1) % 4, t[0], jnp.where(slot == (gap + 2) % 4, t[1], t[2]))

    def merged(t, get):
        d = 4 * t // 3
        edge = (d + 1) * WIDTH - t * LANES
        return get(d) if edge >= LANES else jnp.where(lane < edge, get(d), get(d + 1))

    spans = [slice(t * LANES, (t + 1) * LANES) for t in range(TILES)]
    for t, span in enumerate(spans):
        h = merged(t, lambda d: x_ref[d, 12])
        for l in range(OWN):
            dp_ref[l, :, span] = h
    for f, ref in enumerate((u_ref, v_ref, tr_ref, th_ref)):
        last = [fourth(d, f) for d in range(GROUP)]
        for t, span in enumerate(spans):
            for l in range(3):
                ref[l, :, span] = merged(t, lambda d: x_ref[d, 3 * f + l])
            ref[3, :, span] = merged(t, lambda d: last[d])


def unpack(x):
    shape = jax.ShapeDtypeStruct((OWN, ROWS, TILES * LANES), jnp.float32)
    return pl.pallas_call(
        unpack_kernel,
        out_shape=(shape,) * 5,
        in_specs=[IN_VMEM],
        out_specs=(IN_VMEM,) * 5,
        compiler_params=GRANT,
        name="unpack",
    )(*near(x))


def body(dp, u, v, th, tr, cn, ce):
    lats = lax.axis_size("lat")
    last = (lax.axis_index("lat") == lats - 1).astype(jnp.int32).reshape(1)
    gap = ((3 * lax.axis_index("lev") + 3) % 4 + 4 * (1 - lax.axis_index("lat") % 2)).astype(jnp.int32).reshape(1)
    swaps = [[(i, i + 1) for i in range(start, lats - 1, 2)] for start in (0, 1)]
    swaps = [pairs + [(b, a) for a, b in pairs] for pairs in swaps]

    def across(x):
        return lax.all_to_all(x, "lev", 0, 0, tiled=True)

    def strips(first, second):
        return lax.ppermute(first, "lat", swaps[0]), lax.ppermute(second, "lat", swaps[1])

    held_a = across(pack(CHUNK_A, "one", last, (dp, th, cn, ce)))
    sent_b = pack(CHUNK_B, "all", last, (dp, u, v, tr))
    x_a, courant, first, second = edges(CHUNK_A, (2, 2), gap, held_a)

    first_a, second_a = strips(first, second)
    x_b, first, second = edges(CHUNK_B, (3,), gap, across(sent_b))
    first_b, second_b = strips(first, second)
    theta, push, halo_c, top, inverse, h, bound = first_columns(gap, x_a, courant, first_a, second_a)
    made = second_columns(gap, bound, x_b, courant, halo_c, push, first_b, second_b, top, inverse, h, theta)
    return tuple(unpack(across(made)))


def solution(mesh):
    spec = P("lev", "lat", None)
    return jax.shard_map(body, mesh=mesh, in_specs=(spec,) * 7, out_specs=(spec,) * 5, check_vma=False)
```
